32 devices in a mesh: lat: 4 (over x, core), lon: 8 (over z, y).
Axes of the slice: x: 2, y: 2, z: 4, core: 2. Of those that a mesh axis runs over, the one named last changes fastest.
Arguments:
- features: float32 [16, 256, 1024], P('lat', None, 'lon'), may hold values from -6 to 6
- basis_panels: float32 [16, 3, 9, 255], P('lat'), may hold values from -0.9 to 0.9
- weights: float32 [9, 256, 256], replicated, may hold values from -0.125 to 0.125
- bias_term: float32 [256], replicated, may hold values from -3 to 3
- widths: int32 [16], P('lat'), may hold values from 4 to 127, as said below
- tap_rows: int32 [16, 3], P('lat'), may hold values from -4 to 4, as said below
Outputs:
- convolved: float32 [16, 256, 1024], P('lat', None, 'lon')
The draws below stay inside these ranges and needn't reach their ends.
Inputs may be any that keep to these rules, and one draw needn't show every extreme that they name: With d = min(i, 15 - i) the distance of row i from the nearer pole, widths[i] is at most min(8 * 16 // (4 * d + 2) + 4, 127), and the first and the last row have the half-width 127. In each aligned block of 4 rows the row nearest a pole has exactly this bound. `tap_rows`: the first row's first tap has the offset -4 and the last row's last tap the offset 4.
All inputs are finite; a program needn't handle non-finite values.
Results may differ from the reference program's by a relative error of at most 0.000062.
Values sent between devices are 32-bit elements; how exact they have to be, the bound alone decides.
No kernel may reach another device: no remote copies, remote signals or barrier semaphores. Data moves between devices by JAX's collectives and lax.ppermute only.
A program may use at most 256 MiB of HBM per device.

```python
import jax
import jax.numpy as jnp
from jax import lax

C = 256
K = 9
TAPS = 3
REACH = 4
ROWS = 4
NLAT = 16
NLON = 1024
WMAX = 127
SPAN = 255


def draw_widths(key, part):
    row_ids = jnp.arange(NLAT, dtype=jnp.int32)
    distance = jnp.minimum(row_ids, NLAT - 1 - row_ids)
    base_width = 8 * NLAT // (4 * distance + 2)
    block_nearest = jnp.repeat(jnp.min(distance.reshape(NLAT // ROWS, ROWS), axis=1), ROWS)
    jitter = jax.random.randint(key, (NLAT,), 0, 5, dtype=jnp.int32)
    jitter = jnp.where(distance == block_nearest, 4, jitter)
    result = jnp.minimum(base_width + jitter, WMAX)
    result = jnp.where(distance == 0, WMAX, result)
    return result.astype(jnp.int32)


def draw_tap_rows(key, part):
    offsets = jax.random.randint(key, (NLAT, TAPS), -REACH, REACH + 1, dtype=jnp.int32)
    offsets = offsets.at[0, 0].set(-REACH)
    offsets = offsets.at[NLAT - 1, TAPS - 1].set(REACH)
    return offsets.astype(jnp.int32)


def block_scale(stream_key, extent, cuts, smallest, high):
    gain, own = 1.0, jax.random.fold_in(stream_key, 6)
    for axis_at, blocks in cuts:
        heights = jnp.exp(jax.random.uniform(jax.random.fold_in(own, axis_at), (blocks,), jnp.float32, smallest / len(cuts), high / len(cuts)))
        gain = gain * jnp.repeat(heights, extent[axis_at] // blocks).reshape([-1 if axis == axis_at else 1 for axis in range(len(extent))])
    return gain


def centred(own_key, dims, width, reach, split=(), held_as=jnp.bfloat16):
    factor_of = block_scale(own_key, dims, split, -0.22, 0.18) if split else 1.0
    array = jax.random.normal(own_key, dims, jnp.float32) * width * factor_of
    return jnp.minimum(jnp.maximum(array, -reach), reach).astype(held_as)


def setup_inputs(seed: int = 0) -> dict:
    arg_keys = jax.random.split(jax.random.key(seed), 7)
    return {
        "features": centred(arg_keys[0], (NLAT, C, NLON), 1.0, 6.0, ((0, 4), (2, 8)), jnp.float32),
        "basis_panels": centred(arg_keys[1], (NLAT, TAPS, K, SPAN), 0.15, 0.9, ((0, 4),), jnp.float32),
        "weights": centred(arg_keys[2], (K, C, C), (C * K) ** -0.5, 0.125, (), jnp.float32),
        "bias_term": centred(arg_keys[3], (C,), 0.5, 3.0, (), jnp.float32),
        "widths": draw_widths(jax.random.fold_in(arg_keys[6], 71), 0),
        "tap_rows": draw_tap_rows(jax.random.fold_in(arg_keys[6], 71), 0),
    }


def reference(features, basis_panels, weights, bias_term, widths, tap_rows):
    half_turn = NLON // 2
    top_rows = jnp.roll(features[:REACH][::-1], -half_turn, axis=2)
    low_rows = jnp.roll(features[-REACH:][::-1], -half_turn, axis=2)
    extended = jnp.concatenate([top_rows, features, low_rows], axis=0)
    offsets = jnp.arange(SPAN, dtype=jnp.int32) - WMAX
    inside_band = jnp.abs(offsets)[None, :] <= widths[:, None]
    masked = jnp.where(inside_band[:, None, None, :], basis_panels, jnp.zeros((), basis_panels.dtype))
    places = jnp.mod(offsets, NLON).astype(jnp.int32)
    kernels = jnp.zeros((NLAT, TAPS, K, NLON), basis_panels.dtype).at[:, :, :, places].set(masked)

    def one_row(row_index):
        chosen = jnp.take(extended, row_index + REACH + tap_rows[row_index], axis=0)
        spectrum = jnp.fft.rfft(chosen, axis=-1)
        response = jnp.fft.rfft(kernels[row_index], axis=-1)
        product = jnp.einsum("tkf,tcf->ckf", jnp.conj(response), spectrum)
        spatial = jnp.fft.irfft(product, n=NLON, axis=-1)
        mixed = jnp.einsum("koc,ckl->ol", weights, spatial, precision=lax.Precision.HIGHEST)
        return mixed + bias_term[:, None]

    return lax.map(one_row, jnp.arange(NLAT, dtype=jnp.int32))
```

```python
import functools

import jax
import jax.numpy as jnp
import numpy as np
from jax import lax
from jax.experimental import pallas as pl
from jax.experimental.pallas import tpu as pltpu
from jax.sharding import PartitionSpec as P

REACH = 4
TILE = 16
VMEM = pl.BlockSpec(memory_space=pltpu.VMEM)
SMEM = pl.BlockSpec(memory_space=pltpu.SMEM)
CONTRACT_LAST = (((1,), (1,)), ((), ()))


def shifted(value, axis, by):
    peers = lax.axis_size(axis)
    return lax.ppermute(value, axis, [(i, (i + by) % peers) for i in range(peers)])


def slot_reach(lat_count, rows, half_width):
    total = lat_count * rows
    reach = [0] * rows
    for block in range(lat_count):
        order = range(rows) if 2 * block < lat_count else reversed(range(rows))
        for slot, row in enumerate(order):
            place = block * rows + row
            distance = min(place, total - 1 - place)
            bound = min(8 * total // (4 * distance + 2) + 4, half_width)
            reach[slot] = max(reach[slot], half_width if distance == 0 else bound)
    return [-(-bound // TILE) * TILE for bound in reach]


def halves(value):
    high = value.astype(jnp.bfloat16)
    return high, (value - high.astype(jnp.float32)).astype(jnp.bfloat16)


def dot_last(left, right):
    return lax.dot_general(left, right, CONTRACT_LAST, preferred_element_type=jnp.float32)


def bands_kernel(reach, taps, half, panel_ref, weight_ref, centre_ref, *rest):
    edge_refs, (high_ref, low_ref) = rest[: len(reach)], rest[len(reach) :]
    columns = centre_ref.shape[2]

    def put(out_ref, where, chunk, first, count, tap):
        spread = jnp.broadcast_to(chunk, (count, 2 * columns))
        turned = pltpu.roll(
            spread, 2 * columns - half + first, axis=1, stride=1, stride_axis=0
        )[:, :columns]
        high, low = halves(turned)
        out_ref[where + (slice(tap * columns, (tap + 1) * columns),)] = high
        out_ref[where + (slice((taps + tap) * columns, (taps + tap + 1) * columns),)] = low

    for slot, width in enumerate(reach):
        for tap in range(taps):
            row = panel_ref[0, slot * taps + tap : slot * taps + tap + 1, :]
            put(centre_ref, (slot, 0, slice(None)), row[:, columns : 3 * columns], 0, columns, tap)
            edge = edge_refs[slot]
            put(edge, (0, slice(0, width)), row[:, 2 * columns :], columns - width, width, tap)
            put(edge, (0, slice(width, 2 * width)), row[:, : 2 * columns], 0, width, tap)
    high, low = halves(weight_ref[0])
    high_ref[...] = high
    low_ref[...] = low


def mixed(scratch_ref, high_ref, low_ref):
    depth = high_ref.shape[1]
    upper = scratch_ref[:, :depth]
    total = dot_last(upper, high_ref[...])
    total += dot_last(scratch_ref[:, depth:], high_ref[...])
    return total + dot_last(upper, low_ref[...])


def correlate(band_ref, spread_ref, low_ref, slot, put):
    basis, lines, depth = band_ref.shape
    band = band_ref[...].reshape(basis * lines, depth)
    total = dot_last(band, spread_ref[slot]) + dot_last(band[:, : depth // 2], low_ref[slot])
    high, low = halves(total)
    for k in range(basis):
        put(k, high[k * lines : (k + 1) * lines], low[k * lines : (k + 1) * lines])


def edges_kernel(reach, taps, code_ref, own, above, below, turned, *rest):
    edge_refs = rest[: len(reach)]
    high_ref, low_ref, left_ref, right_ref, spread_ref, rest_ref, scratch = rest[len(reach) :]
    columns = own.shape[2]
    channels = own.shape[1]
    depth = high_ref.shape[1]

    for slot in range(len(reach)):
        for tap in range(taps):
            at = slot * taps + tap

            def put(source, at=at, slot=slot, tap=tap):
                high, low = halves(source[code_ref[1, at]])
                spread_ref[slot, :, tap * columns : (tap + 1) * columns] = high
                spread_ref[slot, :, (taps + tap) * columns : (taps + tap + 1) * columns] = high
                rest_ref[slot, :, tap * columns : (tap + 1) * columns] = low

            for number, source in enumerate((own, above, below, turned)):
                pl.when(code_ref[0, at] == number)(functools.partial(put, source))

    total = sum(reach)
    start = 0
    for slot, width in enumerate(reach):

        def keep(k, high, low, start=start, width=width):
            lanes = slice(k * channels, (k + 1) * channels)
            lower = slice(depth + k * channels, depth + (k + 1) * channels)
            scratch[start : start + width, lanes] = high[:width]
            scratch[start : start + width, lower] = low[:width]
            scratch[total + start : total + start + width, lanes] = high[width:]
            scratch[total + start : total + start + width, lower] = low[width:]

        correlate(edge_refs[slot], spread_ref, rest_ref, slot, keep)
        start += width
    result = mixed(scratch, high_ref, low_ref)
    left_ref[...] = result[:total]
    right_ref[...] = result[total:]


def centre_kernel(spread_ref, rest_ref, band_ref, high_ref, low_ref, out_ref, scratch):
    rows, _, columns, _ = band_ref.shape
    channels = spread_ref.shape[1]
    depth = high_ref.shape[1]
    for slot in range(rows):

        def keep(k, high, low, slot=slot):
            lines = slice(slot * columns, (slot + 1) * columns)
            scratch[lines, k * channels : (k + 1) * channels] = high
            scratch[lines, depth + k * channels : depth + (k + 1) * channels] = low

        correlate(band_ref.at[slot], spread_ref, rest_ref, slot, keep)
    out_ref[...] = mixed(scratch, high_ref, low_ref).reshape(out_ref.shape)


def join_kernel(reach, order_ref, centre_ref, east_ref, west_ref, bias_ref, out_ref):
    columns = out_ref.shape[2]
    start = 0
    for slot, width in enumerate(reach):
        part = centre_ref[slot] + bias_ref[...]
        east = east_ref[start : start + width]
        west = west_ref[start : start + width]
        if width < columns:
            gap = jnp.zeros((columns - width, part.shape[1]), jnp.float32)
            east = jnp.concatenate([gap, east], axis=0)
            west = jnp.concatenate([west, gap], axis=0)
        out_ref[order_ref[slot]] = (part + east + west).T
        start += width


def per_device(features, basis_panels, weights, bias_term, widths, tap_rows):
    rows, channels, columns = features.shape
    _, taps, basis, span = basis_panels.shape
    outs = weights.shape[1]
    half = (span - 1) // 2
    lat_count, lon_count = lax.axis_size("lat"), lax.axis_size("lon")
    place, last = lax.axis_index("lat"), lat_count - 1
    reach = slot_reach(lat_count, rows, half)

    polar = [
        (block * lon_count + at, block * lon_count + (at + lon_count // 2) % lon_count)
        for block in sorted({0, last})
        for at in range(lon_count)
    ]
    turned = lax.ppermute(features, ("lat", "lon"), polar)
    above = lax.ppermute(features, "lat", [(i, i + 1) for i in range(last)])
    below = lax.ppermute(features, "lat", [(i + 1, i) for i in range(last)])

    slots = jnp.arange(rows, dtype=jnp.int32)
    order = jnp.where(2 * place < lat_count, slots, rows - 1 - slots)
    line = order[:, None] + jnp.where(2 * place < lat_count, tap_rows, tap_rows[::-1])
    line = line.reshape(-1)
    up, down = line < 0, line >= rows
    source = jnp.where(
        up,
        jnp.where(place == 0, 3, 1),
        jnp.where(down, jnp.where(place == last, 3, 2), 0),
    )
    row = jnp.where(
        up,
        jnp.where(place == 0, -1 - line, rows + line),
        jnp.where(down, jnp.where(place == last, 2 * rows - 1 - line, line - rows), line),
    )
    codes = jnp.stack([source, row]).astype(jnp.int32)

    offsets = jnp.abs(jnp.arange(span, dtype=jnp.int32) - half)
    masked = jnp.where(offsets <= widths[:, None, None, None], basis_panels, 0.0)
    masked = jnp.where(2 * place < lat_count, masked, masked[::-1])
    masked = jnp.pad(masked, ((0, 0),) * 3 + ((columns, 3 * columns - span),))
    panels = masked.transpose(2, 0, 1, 3).reshape(basis, rows * taps, 4 * columns)

    bands = pl.pallas_call(
        functools.partial(bands_kernel, reach, taps, half),
        grid=(basis,),
        in_specs=[
            pl.BlockSpec((1, rows * taps, 4 * columns), lambda k: (k, 0, 0)),
            pl.BlockSpec((1, outs, channels), lambda k: (k, 0, 0)),
        ],
        out_specs=[pl.BlockSpec((rows, 1, columns, 2 * taps * columns), lambda k: (0, k, 0, 0))]
        + [
            pl.BlockSpec((1, 2 * width, 2 * taps * columns), lambda k: (k, 0, 0))
            for width in reach
        ]
        + [pl.BlockSpec((outs, channels), lambda k: (0, k))] * 2,
        out_shape=[
            jax.ShapeDtypeStruct((rows, basis, columns, 2 * taps * columns), jnp.bfloat16)
        ]
        + [
            jax.ShapeDtypeStruct((basis, 2 * width, 2 * taps * columns), jnp.bfloat16)
            for width in reach
        ]
        + [jax.ShapeDtypeStruct((outs, basis * channels), jnp.bfloat16)] * 2,
        name="bands",
    )(panels, weights)
    centre_band, edge_bands, (high, low) = bands[0], bands[1 : rows + 1], bands[rows + 1 :]

    edge = jax.ShapeDtypeStruct((sum(reach), outs), jnp.float32)
    to_west, to_east, spread, spread_low = pl.pallas_call(
        functools.partial(edges_kernel, reach, taps),
        in_specs=[SMEM] + [VMEM] * (6 + rows),
        out_specs=[VMEM] * 4,
        out_shape=[
            edge,
            edge,
            jax.ShapeDtypeStruct((rows, channels, 2 * taps * columns), jnp.bfloat16),
            jax.ShapeDtypeStruct((rows, channels, taps * columns), jnp.bfloat16),
        ],
        scratch_shapes=[pltpu.VMEM((2 * sum(reach), 2 * basis * channels), jnp.bfloat16)],
        name="edges",
    )(codes, features, above, below, turned, *edge_bands, high, low)

    from_east = shifted(to_west, "lon", -1)
    from_west = shifted(to_east, "lon", 1)

    centre = pl.pallas_call(
        centre_kernel,
        in_specs=[VMEM] * 5,
        out_specs=VMEM,
        out_shape=jax.ShapeDtypeStruct((rows, columns, outs), jnp.float32),
        scratch_shapes=[pltpu.VMEM((rows * columns, 2 * basis * channels), jnp.bfloat16)],
        name="centre",
    )(spread, spread_low, centre_band, high, low)

    return pl.pallas_call(
        functools.partial(join_kernel, reach),
        in_specs=[SMEM] + [VMEM] * 4,
        out_specs=VMEM,
        out_shape=jax.ShapeDtypeStruct((rows, outs, columns), jnp.float32),
        name="join",
    )(order, centre, from_east, from_west, bias_term[None, :])


def solution(mesh):
    return jax.shard_map(
        per_device,
        mesh=mesh,
        in_specs=(
            P("lat", None, "lon"),
            P("lat", None, None, None),
            P(),
            P(),
            P("lat"),
            P("lat", None),
        ),
        out_specs=P("lat", None, "lon"),
        check_vma=False,
    )
```
